32 devices in a mesh: groups: 2 (over x), tm: 16 (over z, y, core).
Axes of the slice: x: 2, y: 2, z: 4, core: 2. Of those that a mesh axis runs over, the one named last changes fastest.
Arguments:
- signal: float32 [2, 8192], P('groups', 'tm'), parts along dimension 0, may hold values from -6 to 6
- codes: bfloat16 [2, 1024, 8192], P('groups', None, 'tm'), parts along dimension 0, may hold values from -6 to 6
- dictionary: float32 [1024, 512], P('tm'), may hold values from -6 to 6
- thresholds: float32 [1024], replicated, may hold values from 0.02 to 0.2
Outputs:
- codes_out: bfloat16 [2, 1024, 8192], P('groups', None, 'tm'), parts along dimension 0
- dictionary_out: float32 [2048, 512], P(('groups', 'tm')), parts along dimension 0
- residual_out: float32 [2, 8192], P('groups', 'tm'), parts along dimension 0
The draws below stay inside these ranges and needn't reach their ends.
There are 2 independent parts, one for each index of `groups`. The reference program is written for one: setup_inputs(seed, part) draws one part's arguments, and reference() takes and returns one part's arrays. A program takes and returns all parts, laid end to end along the dimension named above; an argument that names none is the same for every part. Nothing has to cross between parts.
All inputs are finite; a program needn't handle non-finite values.
Results may differ from the reference program's by a relative error of at most 0.0072.
Values may be sent and summed in bfloat16 or wider, within the bound.
A program may use at most 64 MiB of HBM per device.

```python
import math
import jax
import jax.numpy as jnp
from jax import lax

C = 1
K = 1024
L = 512
ITERS = 2
T_SIZE = 8192


def raised(values, key, source, target, parts, factor):
    def block_of(axis_at):
        return (jnp.arange(values.shape[axis_at]) // (values.shape[axis_at] // parts)).reshape((-1,) + (1,) * (values.ndim - 1 - axis_at))

    near = jax.random.permutation(key, parts)[block_of(target)]
    second = (block_of(target) + parts // 2) % parts
    return jnp.where((block_of(source) == near) | (block_of(source) == second), factor * values, values)


def level_of(key, shape, shards, low, high):
    level, own = 1.0, jax.random.fold_in(key, 6)
    for dim, shards_of in shards:
        steps = jnp.exp(jax.random.uniform(jax.random.fold_in(own, dim), (shards_of,), jnp.float32, low / len(shards), high / len(shards)))
        level = level * jnp.repeat(steps, shape[dim] // shards_of).reshape([-1 if axis == dim else 1 for axis in range(len(shape))])
    return level


def scatter_about(key, extent, deviation, most, shards=(), kind=jnp.bfloat16):
    level = level_of(key, extent, shards, -0.22, 0.18) if shards else 1.0
    values = jax.random.normal(key, extent, jnp.float32) * deviation * level
    return jnp.minimum(jnp.maximum(values, -most), most).astype(kind)


def noise_with(key, extent, width, limit, pieces, heavy, dtype=jnp.bfloat16):
    drawn = width * jax.random.normal(key, extent, jnp.float32)
    if pieces:
        drawn = drawn * level_of(key, extent, pieces, -0.22, 0.18)
    return jnp.clip(raised(drawn, jax.random.fold_in(key, 3), *heavy), -limit, limit).astype(dtype)


def setup_inputs(seed: int = 0, part: int = 0) -> dict:
    keys = jax.random.split(jax.random.key(seed), 5)
    own_keys = jax.random.split(jax.random.fold_in(keys[4], part), 5)
    signal = scatter_about(own_keys[0], (C, T_SIZE), 1.0, 6.0, ((1, 16),), jnp.float32)
    codes = noise_with(own_keys[1], (C, K, T_SIZE), 1.0, 6.0, ((2, 16),), (2, 1, 16, 2.0))
    dictionary = scatter_about(keys[2], (K, L), 1.0, 6.0, ((0, 16),), jnp.float32)
    thresholds = jnp.clip(jnp.exp(jax.random.uniform(keys[3], (K,), jnp.float32, math.log(0.02), math.log(0.2))), 0.02, 0.2)
    return {"signal": signal, "codes": codes, "dictionary": dictionary, "thresholds": thresholds}


CODE_STEP = 6.0
EPSILON = 1e-06

def round_keep(values):
    return lax.optimization_barrier(values.astype(jnp.bfloat16)).astype(jnp.float32)

def reference(signal, codes, dictionary, thresholds):
    factor = (K * L) ** (-0.5)
    current = codes.astype(jnp.float32)
    atoms_now = dictionary
    residual = signal
    numbers = ('NCH', 'OIH', 'NCH')
    for iteration in range(ITERS):
        dict_b = round_keep(atoms_now)
        codes_b = round_keep(current)
        rebuilt = lax.conv_general_dilated(codes_b, dict_b[None, :, ::-1], (1,), [(L - 1, 0)], dimension_numbers=numbers, precision=lax.Precision.HIGHEST)[:, 0, :]
        residual = signal - factor * rebuilt
        rounded = round_keep(residual)
        matched = lax.conv_general_dilated(rounded[:, None, :], dict_b[:, None, :], (1,), [(0, L - 1)], dimension_numbers=numbers, precision=lax.Precision.HIGHEST)
        gradient = factor * lax.conv_general_dilated(rounded[None], jnp.transpose(codes_b, (1, 0, 2)), (1,), [(0, L - 1)], dimension_numbers=numbers, precision=lax.Precision.HIGHEST)[0]
        shrink = current + CODE_STEP * factor * matched
        cutoff = CODE_STEP * thresholds[None, :, None]
        current = jnp.sign(shrink) * jnp.maximum(jnp.abs(shrink) - cutoff, 0.0)
        updated = atoms_now + gradient
        atoms_now = updated / jnp.sqrt(lax.optimization_barrier(jnp.mean(updated * updated, axis=1, keepdims=True)) + EPSILON)
    return (current.astype(jnp.bfloat16), atoms_now, residual)
```

```python
import functools

import jax
import jax.numpy as jnp
from jax import lax
from jax.experimental import pallas as pl
from jax.experimental.pallas import tpu as pltpu
from jax.sharding import PartitionSpec as P

ITERS = 2
CODE_STEP = 6.0
EPSILON = 1e-06
LANES = 128
MESH = pl.DeviceIdType.MESH
BF16, F32 = jnp.bfloat16, jnp.float32


def rolled(x, shift):
    width = x.shape[1]
    shift = shift % width
    return x if shift == 0 else pltpu.roll(x, shift, 1)


def skew_total(lagged):
    lag_count, time_len = lagged.shape
    width = lag_count + time_len
    total = None
    for a in range(LANES // 8):
        part = None
        for b in range(lag_count // LANES):
            block = lagged[pl.ds(b * LANES + a * 8, 8), :]
            pieces = [block]
            if b:
                pieces.insert(0, jnp.zeros((8, b * LANES), F32))
            if width - b * LANES - time_len:
                pieces.append(jnp.zeros((8, width - b * LANES - time_len), F32))
            block = jnp.concatenate(pieces, axis=1)
            part = block if part is None else part + block
        part = rolled(part, 8 * a)
        total = part if total is None else total + part
    out = total[0:1, :]
    for r in range(1, 8):
        out = out + rolled(total, r)[r : r + 1, :]
    return out


def fill_frames(frames, extended):
    lag_count, time_len = frames.shape
    width = extended.shape[1]
    wide = jnp.broadcast_to(extended, (8, width))
    row = lax.broadcasted_iota(jnp.int32, (8, width), 0)
    base = wide
    for r in range(1, 8):
        base = jnp.where(row == r, rolled(wide, width - r), base)
    for a in range(LANES // 16):
        low, high = rolled(base, width - 16 * a), rolled(base, width - 16 * a - 8)
        both = jnp.concatenate([low, high], axis=0).astype(BF16)
        for b in range(lag_count // LANES):
            frames[pl.ds(b * LANES + a * 16, 16), :] = both[:, b * LANES : b * LANES + time_len]


def kernel(
    n, signal_ref, codes_hbm, dictionary_ref, thresholds_ref,
    codes_out_hbm, atoms_ref, residual_ref,
    codes_b, current, atoms_b, lagged, frames, grad, keep,
    over_send, part_send, over_recv, part_recv, signal_next,
    core_send, core_recv, y_send, y_recv, z_send, z_recv,
    local_sem, halo_s, halo_r, sig_s, sig_r,
    az_s, az_r, ay_s, ay_r, ac_s, ac_r,
    gc_s, gc_r, gy_s, gy_r, gz_s, gz_r,
):
    rows, lag_count = dictionary_ref.shape
    atom_count, time_len = codes_b.shape
    factor = (atom_count * lag_count) ** (-0.5)
    nz = n // 4
    me = lax.axis_index("tm")
    core, y, z = me % 2, (me // 2) % 2, me // 4

    def index_of(zz, yy, cc):
        return (zz * 2 + yy) * 2 + cc

    partner = index_of(z, y, 1 - core)
    across = index_of(z, 1 - y, core)
    following, previous = (me + 1) % n, (me + n - 1) % n

    def up(d):
        return (z + d) % nz

    def down(d):
        return (z + nz - d) % nz

    def copy_to(src, dst, send_sem, recv_sem, target):
        return pltpu.make_async_remote_copy(
            src_ref=src, dst_ref=dst, send_sem=send_sem, recv_sem=recv_sem,
            device_id={"tm": target}, device_id_type=MESH,
        )

    load = pltpu.make_async_copy(codes_hbm.at[0], codes_b, local_sem.at[0])
    load.start()

    barrier = pltpu.get_barrier_semaphore()
    for target in [partner, across, following, previous] + [index_of(up(d), y, core) for d in range(1, nz)]:
        pl.semaphore_signal(barrier, inc=1, device_id={"tm": target}, device_id_type=MESH)
    pl.semaphore_wait(barrier, 4 + nz - 1)

    sent = []

    def start(copy):
        copy.start()
        sent.append(copy)

    def block(it, index):
        return atoms_b.at[it, pl.ds(pl.multiple_of(index * rows, rows), rows), :]

    def gather(it):
        def move(index, send_sem, recv_sem, target):
            return copy_to(block(it, index), block(it, index), send_sem, recv_sem, target)

        for d in range(1, nz):
            start(move(me, az_s.at[it, d], az_r.at[it, d], index_of(up(d), y, core)))
        start(move(me, ay_s.at[it, 0], ay_r.at[it, 0], across))
        start(move(me, ac_s.at[it, 0, 0], ac_r.at[it, 0, 0], partner))
        for d in range(1, nz):
            held = index_of(down(d), y, core)
            move(held, az_s.at[it, d], az_r.at[it, d], me).wait_recv()
            start(move(held, ay_s.at[it, d], ay_r.at[it, d], across))
            start(move(held, ac_s.at[it, d, 0], ac_r.at[it, d, 0], partner))
        for d in range(nz):
            held = index_of(down(d), 1 - y, core)
            move(held, ay_s.at[it, d], ay_r.at[it, d], across).wait_recv()
            start(move(held, ac_s.at[it, d, 1], ac_r.at[it, d, 1], partner))
        for d in range(nz):
            for e in range(2):
                held = index_of(down(d), y if e == 0 else 1 - y, 1 - core)
                move(held, ac_s.at[it, d, e], ac_r.at[it, d, e], partner).wait_recv()

    atoms_ref[...] = dictionary_ref[...]
    block(0, me)[...] = dictionary_ref[...].astype(BF16)
    signal_copy = copy_to(signal_ref, signal_next, sig_s, sig_r, previous)

    @pl.when(me > 0)
    def _():
        signal_copy.start()

    for it in range(ITERS):
        last = it == ITERS - 1
        gather(it)
        if it == 0:
            load.wait()
        lagged[...] = lax.dot_general(
            atoms_b[it], codes_b[...], (((0,), (0,)), ((), ())), preferred_element_type=F32
        )
        summed = skew_total(lagged)
        mine, over = summed[:, :time_len], summed[:, time_len:]
        over_send[it] = over
        part_send[it] = mine
        over_copy = copy_to(over_send.at[it], over_recv.at[it], halo_s.at[it, 0], halo_r.at[it, 0], following)
        part_copy = copy_to(part_send.at[it], part_recv.at[it], halo_s.at[it, 1], halo_r.at[it, 1], previous)

        @pl.when(me < n - 1)
        def _():
            over_copy.start()

        @pl.when(me > 0)
        def _():
            part_copy.start()

        @pl.when(me > 0)
        def _():
            over_copy.wait_recv()

        @pl.when(me == 0)
        def _():
            over_recv[it] = jnp.zeros_like(over)

        @pl.when(me < n - 1)
        def _():
            part_copy.wait_recv()
            if it == 0:
                signal_copy.wait_recv()

        @pl.when(me == n - 1)
        def _():
            part_recv[it] = -over
            if it == 0:
                signal_next[...] = jnp.zeros_like(over)

        residual = signal_ref[...] - factor * (mine + over_recv[it])
        ahead = signal_next[...] - factor * (part_recv[it] + over)
        if last:
            residual_ref[...] = residual
        extended = jnp.concatenate([residual, ahead], axis=1).astype(BF16).astype(F32)
        fill_frames(frames, extended)

        order = list(range(1, nz)) + [0]
        layer = 4 * rows

        def own(d, yy, cc):
            return grad[d, pl.ds(pl.multiple_of((yy * 2 + cc) * rows, rows), rows), :]

        core_copies, y_copies, z_copies = {}, {}, {}
        for d in order:
            picked = pl.ds(pl.multiple_of(up(d) * layer, layer), layer)
            grad[d] = jnp.dot(codes_b[picked, :], frames[...], preferred_element_type=F32)
            core_send[it, d, 0] = own(d, y, 1 - core).astype(BF16)
            core_send[it, d, 1] = own(d, 1 - y, 1 - core).astype(BF16)
            core_copies[d] = copy_to(
                core_send.at[it, d], core_recv.at[it, d], gc_s.at[it, d], gc_r.at[it, d], partner
            )
            start(core_copies[d])
        for d in order:
            core_copies[d].wait_recv()
            y_send[it, d] = (own(d, 1 - y, core) + core_recv[it, d, 1].astype(F32)).astype(BF16)
            keep[d] = own(d, y, core) + core_recv[it, d, 0].astype(F32)
            y_copies[d] = copy_to(y_send.at[it, d], y_recv.at[it, d], gy_s.at[it, d], gy_r.at[it, d], across)
            start(y_copies[d])

        step_rows = min(256, atom_count)

        def advance(i, carry):
            picked = pl.ds(pl.multiple_of(i * step_rows, step_rows), step_rows)
            matched = jnp.dot(atoms_b[it, picked, :], frames[...], preferred_element_type=F32)
            before = codes_b[picked, :].astype(F32) if it == 0 else current[picked, :]
            shrink = before + (CODE_STEP * factor) * matched
            cutoff = CODE_STEP * thresholds_ref[picked, :]
            after = shrink - jnp.minimum(jnp.maximum(shrink, -cutoff), cutoff)
            if not last:
                current[picked, :] = after
            codes_b[picked, :] = after.astype(BF16)
            return carry

        lax.fori_loop(0, atom_count // step_rows, advance, 0)
        if last:
            store = pltpu.make_async_copy(codes_b, codes_out_hbm.at[0], local_sem.at[1])
            store.start()

        for d in order:
            y_copies[d].wait_recv()
            keep[d] = keep[d] + y_recv[it, d].astype(F32)
            if d:
                z_send[it, d] = keep[d].astype(BF16)
                z_copies[d] = copy_to(
                    z_send.at[it, d], z_recv.at[it, d], gz_s.at[it, d], gz_r.at[it, d], index_of(up(d), y, core)
                )
                start(z_copies[d])
        total = keep[0]
        for d in range(1, nz):
            z_copies[d].wait_recv()
            total = total + z_recv[it, d].astype(F32)
        updated = atoms_ref[...] + factor * total
        fresh = updated / jnp.sqrt(jnp.mean(updated * updated, axis=1, keepdims=True) + EPSILON)
        atoms_ref[...] = fresh
        if not last:
            block(it + 1, me)[...] = fresh.astype(BF16)

        @pl.when(me < n - 1)
        def _():
            over_copy.wait_send()

        @pl.when(me > 0)
        def _():
            part_copy.wait_send()

    @pl.when(me > 0)
    def _():
        signal_copy.wait_send()

    for copy in sent:
        copy.wait_send()
    store.wait()


def on_device(n, signal, codes, dictionary, thresholds):
    _, atom_count, time_len = codes.shape
    rows, lag_count = dictionary.shape
    nz = n // 4
    vmem, dma = pltpu.VMEM, pltpu.SemaphoreType.DMA
    inside = pl.BlockSpec(memory_space=pltpu.VMEM)
    outside = pl.BlockSpec(memory_space=pl.ANY)
    piece = (rows, lag_count)
    return tuple(
        pl.pallas_call(
            functools.partial(kernel, n),
            name="learn",
            out_shape=(
                jax.ShapeDtypeStruct(codes.shape, BF16),
                jax.ShapeDtypeStruct(piece, F32),
                jax.ShapeDtypeStruct(signal.shape, F32),
            ),
            in_specs=[inside, outside, inside, inside],
            out_specs=(outside, inside, inside),
            scratch_shapes=[
                vmem((atom_count, time_len), BF16),
                vmem((atom_count, time_len), F32),
                vmem((ITERS, atom_count, lag_count), BF16),
                vmem((lag_count, time_len), F32),
                vmem((lag_count, time_len), BF16),
                vmem((nz, 4 * rows, lag_count), F32),
                vmem((nz, *piece), F32),
                vmem((ITERS, 1, time_len), F32),
                vmem((ITERS, 1, time_len), F32),
                vmem((ITERS, 1, time_len), F32),
                vmem((ITERS, 1, time_len), F32),
                vmem((1, time_len), F32),
                vmem((ITERS, nz, 2, *piece), BF16),
                vmem((ITERS, nz, 2, *piece), BF16),
                vmem((ITERS, nz, *piece), BF16),
                vmem((ITERS, nz, *piece), BF16),
                vmem((ITERS, nz, *piece), BF16),
                vmem((ITERS, nz, *piece), BF16),
                dma((2,)),
                dma((ITERS, 2)),
                dma((ITERS, 2)),
                dma,
                dma,
                *[dma((ITERS, nz))] * 4,
                *[dma((ITERS, nz, 2))] * 2,
                *[dma((ITERS, nz))] * 6,
            ],
            compiler_params=pltpu.CompilerParams(
                collective_id=0, has_side_effects=True, vmem_limit_bytes=48 * 1024 * 1024
            ),
        )(signal, codes, dictionary, thresholds[:, None])
    )


def solution(mesh):
    return jax.shard_map(
        functools.partial(on_device, mesh.shape["tm"]),
        mesh=mesh,
        in_specs=(P("groups", "tm"), P("groups", None, "tm"), P("tm", None), P()),
        out_specs=(P("groups", None, "tm"), P(("groups", "tm"), None), P("groups", "tm")),
        check_vma=False,
    )
```

```python
import functools

import jax
import jax.numpy as jnp
from jax import lax
from jax.experimental import pallas as pl
from jax.experimental.pallas import tpu as pltpu
from jax.sharding import PartitionSpec as P

ITERS = 2
CODE_STEP = 6.0
EPSILON = 1e-06
LANES = 128
MESH = pl.DeviceIdType.MESH
BF16, F32 = jnp.bfloat16, jnp.float32


PIECES = 2


def pieces_of(rows):
    return max(1, min(PIECES, rows // 16))


def rolled(x, shift):
    width = x.shape[1]
    shift = shift % width
    return x if shift == 0 else pltpu.roll(x, shift, 1)


def skew_total(lagged):
    lag_count, time_len = lagged.shape
    width = lag_count + time_len
    total = None
    for a in range(LANES // 8):
        part = None
        for b in range(lag_count // LANES):
            block = lagged[pl.ds(b * LANES + a * 8, 8), :]
            pieces = [block]
            if b:
                pieces.insert(0, jnp.zeros((8, b * LANES), F32))
            if width - b * LANES - time_len:
                pieces.append(jnp.zeros((8, width - b * LANES - time_len), F32))
            block = jnp.concatenate(pieces, axis=1)
            part = block if part is None else part + block
        part = rolled(part, 8 * a)
        total = part if total is None else total + part
    out = total[0:1, :]
    for r in range(1, 8):
        out = out + rolled(total, r)[r : r + 1, :]
    return out


def fill_frames(frames, extended):
    lag_count, time_len = frames.shape
    width = extended.shape[1]
    wide = jnp.broadcast_to(extended, (8, width))
    row = lax.broadcasted_iota(jnp.int32, (8, width), 0)
    base = wide
    for r in range(1, 8):
        base = jnp.where(row == r, rolled(wide, width - r), base)
    for a in range(LANES // 16):
        low, high = rolled(base, width - 16 * a), rolled(base, width - 16 * a - 8)
        both = jnp.concatenate([low, high], axis=0).astype(BF16)
        for b in range(lag_count // LANES):
            frames[pl.ds(b * LANES + a * 16, 16), :] = both[:, b * LANES : b * LANES + time_len]


def kernel(
    n, signal_hbm, codes_hbm, dictionary_hbm, thresholds_hbm,
    codes_out_hbm, atoms_ref, residual_ref,
    signal_ref, dictionary_ref, thresholds_ref, cutoffs, codes_b, current, atoms_b, lagged, frames, grad, keep,
    over_send, part_send, over_recv, part_recv, signal_next,
    core_send, core_recv, y_send, y_recv, z_send, z_recv,
    local_sem, halo_s, halo_r, sig_s, sig_r,
    az_s, az_r, ay_s, ay_r, ac_s, ac_r,
    gc_s, gc_r, gy_s, gy_r, gz_s, gz_r,
):
    rows, lag_count = dictionary_ref.shape
    atom_count, time_len = codes_b.shape
    factor = (atom_count * lag_count) ** (-0.5)
    nz = n // 4
    me = lax.axis_index("tm")
    core, y, z = me % 2, (me // 2) % 2, me // 4

    def index_of(zz, yy, cc):
        return (zz * 2 + yy) * 2 + cc

    partner = index_of(z, y, 1 - core)
    across = index_of(z, 1 - y, core)
    following, previous = (me + 1) % n, (me + n - 1) % n

    upper = (z * 2) // nz

    def layer_at(d):
        if d == nz - 1:
            return z
        fall, rise = nz - 1 - d, d
        fall = fall - (z - fall + nz) // nz
        rise = rise + (rise - z + nz) // nz
        return upper * rise + (1 - upper) * fall

    layers = [layer_at(d) for d in range(nz)]
    others = range(nz - 1)
    mine_at = nz - 1

    def copy_to(src, dst, send_sem, recv_sem, target):
        return pltpu.make_async_remote_copy(
            src_ref=src, dst_ref=dst, send_sem=send_sem, recv_sem=recv_sem,
            device_id={"tm": target}, device_id_type=MESH,
        )

    loads = [
        pltpu.make_async_copy(dictionary_hbm, dictionary_ref, local_sem.at[1]),
        pltpu.make_async_copy(signal_hbm, signal_ref, local_sem.at[2]),
        pltpu.make_async_copy(thresholds_hbm, thresholds_ref, local_sem.at[3]),
        pltpu.make_async_copy(codes_hbm.at[0], codes_b, local_sem.at[0]),
    ]
    for load in loads:
        load.start()

    barrier = pltpu.get_barrier_semaphore()
    for target in [partner, across, following, previous] + [index_of(layers[d], y, core) for d in others]:
        pl.semaphore_signal(barrier, inc=1, device_id={"tm": target}, device_id_type=MESH)
    pl.semaphore_wait(barrier, 4 + nz - 1)

    sent = []

    def start(copy):
        copy.start()
        sent.append(copy)

    def block(it, index):
        return atoms_b.at[it, pl.ds(pl.multiple_of(index * rows, rows), rows), :]

    pieces = pieces_of(rows)
    part = rows // pieces

    def gather(it):
        def move(index, q, send_sem, recv_sem, target):
            held = atoms_b.at[it, pl.ds(pl.multiple_of(index * rows + q * part, part), part), :]
            return copy_to(held, held, send_sem, recv_sem, target)

        def to_across(index, d, q):
            return move(index, q, ay_s.at[it, d, q], ay_r.at[it, d, q], across)

        def to_partner(index, d, e, q):
            return move(index, q, ac_s.at[it, d, e, q], ac_r.at[it, d, e, q], partner)

        for q in range(pieces):
            for d in others:
                start(move(me, q, az_s.at[it, d, q], az_r.at[it, z, q], index_of(layers[d], y, core)))
            start(to_across(me, mine_at, q))
        for q in range(pieces):
            start(to_partner(me, mine_at, 0, q))
        for q in range(pieces):
            for d in others:
                held = index_of(layers[d], y, core)
                move(held, q, az_s.at[it, d, q], az_r.at[it, layers[d], q], across).wait_recv()
                start(to_across(held, d, q))
                start(to_partner(held, d, 0, q))
        for q in range(pieces):
            held = index_of(z, 1 - y, core)
            to_across(held, mine_at, q).wait_recv()
            start(to_partner(held, mine_at, 1, q))
        for q in range(pieces):
            for d in others:
                held = index_of(layers[d], 1 - y, core)
                to_across(held, d, q).wait_recv()
                start(to_partner(held, d, 1, q))
        for d in range(nz):
            for e in range(2):
                for q in range(pieces):
                    held = index_of(layers[d], y if e == 0 else 1 - y, 1 - core)
                    to_partner(held, d, e, q).wait_recv()

    loads[0].wait()
    loads[1].wait()
    atoms_ref[...] = dictionary_ref[...]
    block(0, me)[...] = dictionary_ref[...].astype(BF16)
    signal_copy = copy_to(signal_ref, signal_next, sig_s, sig_r, previous)

    @pl.when(me > 0)
    def _():
        signal_copy.start()

    for it in range(ITERS):
        last = it == ITERS - 1
        gather(it)
        if it == 0:
            loads[2].wait()
            cutoffs[...] = CODE_STEP * jnp.broadcast_to(thresholds_ref[...], (8, atom_count)).T[:, 0:1]
            loads[3].wait()
        lagged[...] = lax.dot_general(
            atoms_b[it], codes_b[...], (((0,), (0,)), ((), ())), preferred_element_type=F32
        )
        summed = skew_total(lagged)
        mine, over = summed[:, :time_len], summed[:, time_len:]
        over_send[it] = over
        part_send[it] = mine
        over_copy = copy_to(over_send.at[it], over_recv.at[it], halo_s.at[it, 0], halo_r.at[it, 0], following)
        part_copy = copy_to(part_send.at[it], part_recv.at[it], halo_s.at[it, 1], halo_r.at[it, 1], previous)

        @pl.when(me < n - 1)
        def _():
            over_copy.start()

        @pl.when(me > 0)
        def _():
            part_copy.start()

        @pl.when(me > 0)
        def _():
            over_copy.wait_recv()

        @pl.when(me == 0)
        def _():
            over_recv[it] = jnp.zeros_like(over)

        @pl.when(me < n - 1)
        def _():
            part_copy.wait_recv()
            if it == 0:
                signal_copy.wait_recv()

        @pl.when(me == n - 1)
        def _():
            part_recv[it] = -over
            if it == 0:
                signal_next[...] = jnp.zeros_like(over)

        residual = signal_ref[...] - factor * (mine + over_recv[it])
        ahead = signal_next[...] - factor * (part_recv[it] + over)
        if last:
            residual_ref[...] = residual
        extended = jnp.concatenate([residual, ahead], axis=1).astype(BF16).astype(F32)
        fill_frames(frames, extended)

        order = range(nz)
        layer = 4 * rows

        def own(d, yy, cc):
            return grad[d, pl.ds(pl.multiple_of((yy * 2 + cc) * rows, rows), rows), :]

        core_copies, y_copies, z_copies = {}, {}, {}
        for d in order:
            picked = pl.ds(pl.multiple_of(layers[d] * layer, layer), layer)
            grad[d] = jnp.dot(codes_b[picked, :], frames[...], preferred_element_type=F32)
            core_send[it, d, 0] = own(d, y, 1 - core).astype(BF16)
            core_send[it, d, 1] = own(d, 1 - y, 1 - core).astype(BF16)
            core_copies[d] = copy_to(
                core_send.at[it, d], core_recv.at[it, d], gc_s.at[it, d], gc_r.at[it, d], partner
            )
            start(core_copies[d])
        step_rows = min(256, atom_count)
        steps = atom_count // step_rows

        def advance(i):
            picked = pl.ds(i * step_rows, step_rows)
            matched = jnp.dot(atoms_b[it, picked, :], frames[...], preferred_element_type=F32)
            before = codes_b[picked, :].astype(F32) if it == 0 else current[picked, :]
            shrink = before + (CODE_STEP * factor) * matched
            cutoff = cutoffs[picked, :]
            after = shrink - jnp.minimum(jnp.maximum(shrink, -cutoff), cutoff)
            if not last:
                current[picked, :] = after
            codes_b[picked, :] = after.astype(BF16)

        advance(0)
        for d in order:
            core_copies[d].wait_recv()
            y_send[it, d] = (own(d, 1 - y, core) + core_recv[it, d, 1].astype(F32)).astype(BF16)
            keep[d] = own(d, y, core) + core_recv[it, d, 0].astype(F32)
            y_copies[d] = copy_to(y_send.at[it, d], y_recv.at[it, d], gy_s.at[it, d], gy_r.at[it, d], across)
            start(y_copies[d])

        for i in range(1, steps - 1):
            advance(i)
        for d in order:
            y_copies[d].wait_recv()
            keep[d] = keep[d] + y_recv[it, d].astype(F32)
            if d != mine_at:
                z_send[it, d] = keep[d].astype(BF16)
                z_copies[d] = copy_to(
                    z_send.at[it, d], z_recv.at[it, z], gz_s.at[it, d], gz_r.at[it, z], index_of(layers[d], y, core)
                )
                start(z_copies[d])
        advance(steps - 1)
        if last:
            store = pltpu.make_async_copy(codes_b, codes_out_hbm.at[0], local_sem.at[1])
            store.start()
        total = keep[mine_at]
        for d in others:
            copy_to(
                z_send.at[it, d], z_recv.at[it, layers[d]], gz_s.at[it, d], gz_r.at[it, layers[d]], across
            ).wait_recv()
            total = total + z_recv[it, layers[d]].astype(F32)
        updated = atoms_ref[...] + factor * total
        fresh = updated / jnp.sqrt(jnp.mean(updated * updated, axis=1, keepdims=True) + EPSILON)
        atoms_ref[...] = fresh
        if not last:
            block(it + 1, me)[...] = fresh.astype(BF16)

        @pl.when(me < n - 1)
        def _():
            over_copy.wait_send()

        @pl.when(me > 0)
        def _():
            part_copy.wait_send()

    @pl.when(me > 0)
    def _():
        signal_copy.wait_send()

    for copy in sent:
        copy.wait_send()
    store.wait()


def on_device(n, signal, codes, dictionary, thresholds):
    _, atom_count, time_len = codes.shape
    rows, lag_count = dictionary.shape
    nz = n // 4
    vmem, dma = pltpu.VMEM, pltpu.SemaphoreType.DMA
    inside = pl.BlockSpec(memory_space=pltpu.VMEM)
    outside = pl.BlockSpec(memory_space=pltpu.HBM)
    piece = (rows, lag_count)
    return tuple(
        pl.pallas_call(
            functools.partial(kernel, n),
            name="learn",
            out_shape=(
                jax.ShapeDtypeStruct(codes.shape, BF16),
                jax.ShapeDtypeStruct(piece, F32),
                jax.ShapeDtypeStruct(signal.shape, F32),
            ),
            in_specs=[outside] * 4,
            out_specs=(pl.BlockSpec(memory_space=pl.ANY), inside, inside),
            scratch_shapes=[
                vmem(signal.shape, F32),
                vmem(piece, F32),
                vmem((1, atom_count), F32),
                vmem((atom_count, 1), F32),
                vmem((atom_count, time_len), BF16),
                vmem((atom_count, time_len), F32),
                vmem((ITERS, atom_count, lag_count), BF16),
                vmem((lag_count, time_len), F32),
                vmem((lag_count, time_len), BF16),
                vmem((nz, 4 * rows, lag_count), F32),
                vmem((nz, *piece), F32),
                vmem((ITERS, 1, time_len), F32),
                vmem((ITERS, 1, time_len), F32),
                vmem((ITERS, 1, time_len), F32),
                vmem((ITERS, 1, time_len), F32),
                vmem((1, time_len), F32),
                vmem((ITERS, nz, 2, *piece), BF16),
                vmem((ITERS, nz, 2, *piece), BF16),
                vmem((ITERS, nz, *piece), BF16),
                vmem((ITERS, nz, *piece), BF16),
                vmem((ITERS, nz, *piece), BF16),
                vmem((ITERS, nz, *piece), BF16),
                dma((4,)),
                dma((ITERS, 2)),
                dma((ITERS, 2)),
                dma,
                dma,
                *[dma((ITERS, nz, pieces_of(rows)))] * 4,
                *[dma((ITERS, nz, 2, pieces_of(rows)))] * 2,
                *[dma((ITERS, nz))] * 6,
            ],
            compiler_params=pltpu.CompilerParams(
                collective_id=0, has_side_effects=True, vmem_limit_bytes=66_000_000
            ),
        )(signal, codes, dictionary, thresholds[None, :])
    )


def solution(mesh):
    return jax.shard_map(
        functools.partial(on_device, mesh.shape["tm"]),
        mesh=mesh,
        in_specs=(P("groups", "tm"), P("groups", None, "tm"), P("tm", None), P()),
        out_specs=(P("groups", None, "tm"), P(("groups", "tm"), None), P("groups", "tm")),
        check_vma=False,
    )
```

```python
import functools

import jax
import jax.numpy as jnp
from jax import lax
from jax.experimental import pallas as pl
from jax.experimental.pallas import tpu as pltpu
from jax.sharding import PartitionSpec as P

ITERS = 2
CODE_STEP = 6.0
EPSILON = 1e-06
LANES = 128
MESH = pl.DeviceIdType.MESH
BF16, F32 = jnp.bfloat16, jnp.float32


PIECES = 2


def pieces_of(rows):
    return max(1, min(PIECES, rows // 16))


def rolled(x, shift):
    width = x.shape[1]
    shift = shift % width
    return x if shift == 0 else pltpu.roll(x, shift, 1)


def skew_total(lagged):
    lag_count, time_len = lagged.shape
    width = lag_count + time_len
    total = None
    for a in range(LANES // 8):
        part = None
        for b in range(lag_count // LANES):
            block = lagged[pl.ds(b * LANES + a * 8, 8), :]
            pieces = [block]
            if b:
                pieces.insert(0, jnp.zeros((8, b * LANES), F32))
            if width - b * LANES - time_len:
                pieces.append(jnp.zeros((8, width - b * LANES - time_len), F32))
            block = jnp.concatenate(pieces, axis=1)
            part = block if part is None else part + block
        part = rolled(part, 8 * a)
        total = part if total is None else total + part
    out = total[0:1, :]
    for r in range(1, 8):
        out = out + rolled(total, r)[r : r + 1, :]
    return out


def fill_frames(frames, extended):
    lag_count, time_len = frames.shape
    width = extended.shape[1]
    wide = jnp.broadcast_to(extended, (8, width))
    row = lax.broadcasted_iota(jnp.int32, (8, width), 0)
    base = wide
    for r in range(1, 8):
        base = jnp.where(row == r, rolled(wide, width - r), base)
    for a in range(LANES // 16):
        low, high = rolled(base, width - 16 * a), rolled(base, width - 16 * a - 8)
        both = jnp.concatenate([low, high], axis=0).astype(BF16)
        for b in range(lag_count // LANES):
            frames[pl.ds(b * LANES + a * 16, 16), :] = both[:, b * LANES : b * LANES + time_len]


def kernel(
    n, signal_hbm, codes_hbm, dictionary_hbm, thresholds_hbm,
    codes_out_hbm, atoms_ref, residual_ref,
    signal_ref, dictionary_ref, thresholds_ref, cutoffs, codes_b, current, atoms_b, lagged, frames, grad, keep,
    over_send, part_send, over_recv, part_recv, signal_next,
    core_send, core_recv, y_send, y_recv, z_send, z_recv,
    local_sem, halo_s, halo_r, sig_s, sig_r,
    az_s, az_r, ay_s, ay_r, ac_s, ac_r,
    gc_s, gc_r, gy_s, gy_r, gz_s, gz_r,
):
    rows, lag_count = dictionary_ref.shape
    atom_count, time_len = codes_b.shape
    factor = (atom_count * lag_count) ** (-0.5)
    nz = n // 4
    me = lax.axis_index("tm")
    core, y, z = me % 2, (me // 2) % 2, me // 4

    def index_of(zz, yy, cc):
        return (zz * 2 + yy) * 2 + cc

    partner = index_of(z, y, 1 - core)
    across = index_of(z, 1 - y, core)
    following, previous = (me + 1) % n, (me + n - 1) % n

    upper = (z * 2) // nz

    def layer_at(d):
        if d == nz - 1:
            return z
        fall, rise = nz - 1 - d, d
        fall = fall - (z - fall + nz) // nz
        rise = rise + (rise - z + nz) // nz
        return upper * rise + (1 - upper) * fall

    layers = [layer_at(d) for d in range(nz)]
    others = range(nz - 1)
    mine_at = nz - 1

    def copy_to(src, dst, send_sem, recv_sem, target):
        return pltpu.make_async_remote_copy(
            src_ref=src, dst_ref=dst, send_sem=send_sem, recv_sem=recv_sem,
            device_id={"tm": target}, device_id_type=MESH,
        )

    loads = [
        pltpu.make_async_copy(dictionary_hbm, dictionary_ref, local_sem.at[1]),
        pltpu.make_async_copy(signal_hbm, signal_ref, local_sem.at[2]),
        pltpu.make_async_copy(thresholds_hbm, thresholds_ref, local_sem.at[3]),
        pltpu.make_async_copy(codes_hbm.at[0], codes_b, local_sem.at[0]),
    ]
    for load in loads:
        load.start()

    barrier = pltpu.get_barrier_semaphore()
    for target in [partner, across, following, previous] + [index_of(layers[d], y, core) for d in others]:
        pl.semaphore_signal(barrier, inc=1, device_id={"tm": target}, device_id_type=MESH)
    pl.semaphore_wait(barrier, 4 + nz - 1)

    sent = []

    def start(copy):
        copy.start()
        sent.append(copy)

    def block(it, index):
        return atoms_b.at[it, pl.ds(pl.multiple_of(index * rows, rows), rows), :]

    pieces = pieces_of(rows)
    part = rows // pieces

    def gather(it):
        def move(index, q, send_sem, recv_sem, target):
            held = atoms_b.at[it, pl.ds(pl.multiple_of(index * rows + q * part, part), part), :]
            return copy_to(held, held, send_sem, recv_sem, target)

        def to_across(index, d, q):
            return move(index, q, ay_s.at[it, d, q], ay_r.at[it, d, q], across)

        def to_partner(index, d, e, q):
            return move(index, q, ac_s.at[it, d, e, q], ac_r.at[it, d, e, q], partner)

        for q in range(pieces):
            for d in others:
                start(move(me, q, az_s.at[it, d, q], az_r.at[it, z, q], index_of(layers[d], y, core)))
            start(to_across(me, mine_at, q))
        for q in range(pieces):
            start(to_partner(me, mine_at, 0, q))
        for q in range(pieces):
            for d in others:
                held = index_of(layers[d], y, core)
                move(held, q, az_s.at[it, d, q], az_r.at[it, layers[d], q], across).wait_recv()
                start(to_across(held, d, q))
                start(to_partner(held, d, 0, q))
        for q in range(pieces):
            held = index_of(z, 1 - y, core)
            to_across(held, mine_at, q).wait_recv()
            start(to_partner(held, mine_at, 1, q))
        for q in range(pieces):
            for d in others:
                held = index_of(layers[d], 1 - y, core)
                to_across(held, d, q).wait_recv()
                start(to_partner(held, d, 1, q))
        for d in range(nz):
            for e in range(2):
                for q in range(pieces):
                    held = index_of(layers[d], y if e == 0 else 1 - y, 1 - core)
                    to_partner(held, d, e, q).wait_recv()

    loads[0].wait()
    loads[1].wait()
    atoms_ref[...] = dictionary_ref[...]
    block(0, me)[...] = dictionary_ref[...].astype(BF16)
    signal_copy = copy_to(signal_ref, signal_next, sig_s, sig_r, previous)

    @pl.when(me > 0)
    def _():
        signal_copy.start()

    for it in range(ITERS):
        last = it == ITERS - 1
        gather(it)
        if it == 0:
            loads[2].wait()
            cutoffs[...] = CODE_STEP * jnp.broadcast_to(thresholds_ref[...], (8, atom_count)).T[:, 0:1]
            loads[3].wait()
        lagged[...] = lax.dot_general(
            atoms_b[it], codes_b[...], (((0,), (0,)), ((), ())), preferred_element_type=F32
        )
        summed = skew_total(lagged)
        mine, over = summed[:, :time_len], summed[:, time_len:]
        over_send[it] = over
        part_send[it] = mine
        over_copy = copy_to(over_send.at[it], over_recv.at[it], halo_s.at[it, 0], halo_r.at[it, 0], following)
        part_copy = copy_to(part_send.at[it], part_recv.at[it], halo_s.at[it, 1], halo_r.at[it, 1], previous)

        @pl.when(me < n - 1)
        def _():
            over_copy.start()

        @pl.when(me > 0)
        def _():
            part_copy.start()

        @pl.when(me > 0)
        def _():
            over_copy.wait_recv()

        @pl.when(me == 0)
        def _():
            over_recv[it] = jnp.zeros_like(over)

        @pl.when(me < n - 1)
        def _():
            part_copy.wait_recv()
            if it == 0:
                signal_copy.wait_recv()

        @pl.when(me == n - 1)
        def _():
            part_recv[it] = -over
            if it == 0:
                signal_next[...] = jnp.zeros_like(over)

        residual = signal_ref[...] - factor * (mine + over_recv[it])
        ahead = signal_next[...] - factor * (part_recv[it] + over)
        if last:
            residual_ref[...] = residual
        extended = jnp.concatenate([residual, ahead], axis=1).astype(BF16).astype(F32)
        fill_frames(frames, extended)

        order = range(nz)
        layer = 4 * rows

        def own(d, yy, cc):
            return grad[d, pl.ds(pl.multiple_of((yy * 2 + cc) * rows, rows), rows), :]

        core_copies, y_copies, z_copies = {}, {}, {}
        for d in order:
            picked = pl.ds(pl.multiple_of(layers[d] * layer, layer), layer)
            grad[d] = jnp.dot(codes_b[picked, :], frames[...], preferred_element_type=F32)
            core_send[it, d, 0] = own(d, y, 1 - core).astype(BF16)
            core_send[it, d, 1] = own(d, 1 - y, 1 - core).astype(BF16)
            core_copies[d] = copy_to(
                core_send.at[it, d], core_recv.at[it, d], gc_s.at[it, d], gc_r.at[it, d], partner
            )
            start(core_copies[d])
        step_rows = min(256, atom_count)
        steps = atom_count // step_rows

        def advance(i):
            picked = pl.ds(i * step_rows, step_rows)
            matched = jnp.dot(atoms_b[it, picked, :], frames[...], preferred_element_type=F32)
            before = codes_b[picked, :].astype(F32) if it == 0 else current[picked, :]
            shrink = before + (CODE_STEP * factor) * matched
            cutoff = cutoffs[picked, :]
            after = shrink - jnp.minimum(jnp.maximum(shrink, -cutoff), cutoff)
            if not last:
                current[picked, :] = after
            codes_b[picked, :] = after.astype(BF16)

        advance(0)
        for d in order:
            core_copies[d].wait_recv()
            y_send[it, d] = (own(d, 1 - y, core) + core_recv[it, d, 1].astype(F32)).astype(BF16)
            keep[d] = own(d, y, core) + core_recv[it, d, 0].astype(F32)
            y_copies[d] = copy_to(y_send.at[it, d], y_recv.at[it, d], gy_s.at[it, d], gy_r.at[it, d], across)
            start(y_copies[d])

        for i in range(1, steps - 1):
            advance(i)
        for d in order:
            y_copies[d].wait_recv()
            keep[d] = keep[d] + y_recv[it, d].astype(F32)
            if d != mine_at:
                z_send[it, d] = keep[d].astype(BF16)
                z_copies[d] = copy_to(
                    z_send.at[it, d], z_recv.at[it, z], gz_s.at[it, d], gz_r.at[it, z], index_of(layers[d], y, core)
                )
                start(z_copies[d])
        advance(steps - 1)
        if last:
            store = pltpu.make_async_copy(codes_b, codes_out_hbm.at[0], local_sem.at[1])
            store.start()
        total = keep[mine_at]
        for d in others:
            copy_to(
                z_send.at[it, d], z_recv.at[it, layers[d]], gz_s.at[it, d], gz_r.at[it, layers[d]], across
            ).wait_recv()
            total = total + z_recv[it, layers[d]].astype(F32)
        updated = atoms_ref[...] + factor * total
        fresh = updated / jnp.sqrt(jnp.mean(updated * updated, axis=1, keepdims=True) + EPSILON)
        atoms_ref[...] = fresh
        if not last:
            block(it + 1, me)[...] = fresh.astype(BF16)

        @pl.when(me < n - 1)
        def _():
            over_copy.wait_send()

        @pl.when(me > 0)
        def _():
            part_copy.wait_send()

    @pl.when(me > 0)
    def _():
        signal_copy.wait_send()

    for copy in sent:
        copy.wait_send()
    store.wait()


def on_device(n, signal, codes, dictionary, thresholds):
    _, atom_count, time_len = codes.shape
    rows, lag_count = dictionary.shape
    nz = n // 4
    vmem, dma = pltpu.VMEM, pltpu.SemaphoreType.DMA
    inside = pl.BlockSpec(memory_space=pltpu.VMEM)
    outside = pl.BlockSpec(memory_space=pltpu.HBM)
    piece = (rows, lag_count)
    made = tuple(
        pl.pallas_call(
            functools.partial(kernel, n),
            name="learn",
            out_shape=(
                jax.ShapeDtypeStruct(codes.shape, BF16),
                jax.ShapeDtypeStruct(piece, F32),
                jax.ShapeDtypeStruct(signal.shape, F32),
            ),
            in_specs=[outside] * 4,
            out_specs=(pl.BlockSpec(memory_space=pl.ANY), inside, inside),
            scratch_shapes=[
                vmem(signal.shape, F32),
                vmem(piece, F32),
                vmem((1, atom_count), F32),
                vmem((atom_count, 1), F32),
                vmem((atom_count, time_len), BF16),
                vmem((atom_count, time_len), F32),
                vmem((ITERS, atom_count, lag_count), BF16),
                vmem((lag_count, time_len), F32),
                vmem((lag_count, time_len), BF16),
                vmem((nz, 4 * rows, lag_count), F32),
                vmem((nz, *piece), F32),
                vmem((ITERS, 1, time_len), F32),
                vmem((ITERS, 1, time_len), F32),
                vmem((ITERS, 1, time_len), F32),
                vmem((ITERS, 1, time_len), F32),
                vmem((1, time_len), F32),
                vmem((ITERS, nz, 2, *piece), BF16),
                vmem((ITERS, nz, 2, *piece), BF16),
                vmem((ITERS, nz, *piece), BF16),
                vmem((ITERS, nz, *piece), BF16),
                vmem((ITERS, nz, *piece), BF16),
                vmem((ITERS, nz, *piece), BF16),
                dma((4,)),
                dma((ITERS, 2)),
                dma((ITERS, 2)),
                dma,
                dma,
                *[dma((ITERS, nz, pieces_of(rows)))] * 4,
                *[dma((ITERS, nz, 2, pieces_of(rows)))] * 2,
                *[dma((ITERS, nz))] * 6,
            ],
            compiler_params=pltpu.CompilerParams(
                collective_id=0, has_side_effects=True, vmem_limit_bytes=66_000_000
            ),
        )(signal, codes, dictionary, thresholds[None, :])
    )

    quarter = atom_count // 4

    def publish(codes_ref, atoms_ref, residual_ref, codes_out, atoms_out, residual_out, held, atoms, residual, sem_in, sem_out):
        views = [
            [ref.at[0, pl.ds(i * quarter, quarter), :] for ref in (codes_ref, held, codes_out)] for i in range(4)
        ] + [[atoms_ref, atoms, atoms_out], [residual_ref, residual, residual_out]]
        takes = [pltpu.make_async_copy(view[0], view[1], sem_in.at[i]) for i, view in enumerate(views)]
        puts = [pltpu.make_async_copy(view[1], view[2], sem_out.at[i]) for i, view in enumerate(views)]
        for take in takes:
            take.start()
        for take, put in zip(takes, puts):
            take.wait()
            put.start()
        for put in puts:
            put.wait()

    return tuple(
        pl.pallas_call(
            publish,
            name="publish",
            out_shape=tuple(jax.ShapeDtypeStruct(x.shape, x.dtype) for x in made),
            in_specs=[outside] * 3,
            out_specs=(outside,) * 3,
            scratch_shapes=[*[vmem(x.shape, x.dtype) for x in made], dma((6,)), dma((6,))],
        )(*made)
    )


def solution(mesh):
    return jax.shard_map(
        functools.partial(on_device, mesh.shape["tm"]),
        mesh=mesh,
        in_specs=(P("groups", "tm"), P("groups", None, "tm"), P("tm", None), P()),
        out_specs=(P("groups", None, "tm"), P(("groups", "tm"), None), P("groups", "tm")),
        check_vma=False,
    )
```
